256 devices in a mesh: seq: 32 (over y, z_lo, core), head: 8 (over x, z_hi).
Axes of the slice: x: 4, y: 4, z: 8 (z_hi: 2, z_lo: 4; z = z_hi * 4 + z_lo), core: 2. Of those that a mesh axis runs over, the one named last changes fastest.
Arguments:
- tokens: bfloat16 [131072, 1024], P(('seq', 'head')), may hold values from -32 to 32
- w_qkv: bfloat16 [1024, 3072], P('seq'), may hold values from -0.1875 to 0.1875
- w_out: bfloat16 [1024, 1024], P('seq'), may hold values from -0.1875 to 0.1875
- neighbours: int32 [1024, 12], P('seq'), may hold values from 0 to 1023, as said below
Outputs:
- update: bfloat16 [131072, 1024], P(('seq', 'head'))
The draws below stay inside these ranges and needn't reach their ends.
Inputs may be any that keep to these rules, and one draw needn't show every extreme that they name: Block b has grid coordinates z = b // 16, y = (b // 4) % 4, x = b % 4. Each row lists b itself first, then 11 different blocks among its 26 neighbours at offsets -1, 0, 1 in each coordinate (z taken modulo 1024 // 16, y and x modulo 4).
All inputs are finite; a program needn't handle non-finite values.
Results may differ from the reference program's by a relative error of at most 0.0065.
The reference program's roundings to bfloat16 on the way (of `qkv`, `probs` and `attended`) count: a program that leaves them out, or rounds other values in their place, can miss the bound.
Values may be sent and summed in bfloat16 or wider, within the bound.
A program may use at most 64 MiB of HBM per device.

```python
import math
import jax
import jax.numpy as jnp
import numpy as np
from jax import lax

D = 1024
HEADS = 8
HD = 128
BLK = 128
NBR = 12
PB = 16
NBLK = 1024
TOKENS = 131072


def offset_table():
    rows = []
    for step_z in (-1, 0, 1):
        for step_y in (-1, 0, 1):
            for step_x in (-1, 0, 1):
                if step_z != 0 or step_y != 0 or step_x != 0:
                    rows.append([step_z, step_y, step_x])
    return np.array(rows, dtype=np.int32)


def draw_neighbours(key, part):
    depth = NBLK // PB
    blocks = jnp.arange(NBLK, dtype=jnp.int32)
    coord_z = blocks // PB
    coord_y = blocks // 4 % 4
    coord_x = blocks % 4
    table = jnp.asarray(offset_table())
    scores = jax.random.randint(key, (NBLK, 26), 0, 1 << 20) * 32 + jnp.arange(26, dtype=jnp.int32)
    unused, picks = lax.top_k(scores, NBR - 1)
    chosen = table[picks]
    near_z = jnp.mod(coord_z[:, None] + chosen[:, :, 0], depth)
    near_y = jnp.mod(coord_y[:, None] + chosen[:, :, 1], 4)
    near_x = jnp.mod(coord_x[:, None] + chosen[:, :, 2], 4)
    others = near_z * PB + near_y * 4 + near_x
    return jnp.concatenate([blocks[:, None], others], axis=1).astype(jnp.int32)


def draw_tokens(key, part):
    values = jax.random.normal(key, (TOKENS, D), jnp.float32)
    return jnp.clip(values, -4.0, 4.0).astype(jnp.bfloat16)


def block_scale(rng, dims, cuts, low, high):
    def one(position, blocks):
        heights = jax.random.uniform(jax.random.fold_in(jax.random.fold_in(rng, 6), position), (blocks,), jnp.float32, low / len(cuts), high / len(cuts))
        return jnp.repeat(jnp.exp(heights), dims[position] // blocks).reshape((-1,) + (1,) * (len(dims) - position - 1))

    loudness = one(*cuts[0])
    for cut in cuts[1:]:
        loudness = loudness * one(*cut)
    return loudness


def scatter_about(rng, extent, deviation, most, cuts=(), held_as=jnp.bfloat16):
    drawn = jax.random.normal(rng, extent, jnp.float32) * deviation
    if len(cuts) > 0:
        drawn = block_scale(rng, extent, cuts, -0.22, 0.18) * drawn
    return jnp.clip(drawn, min=-most, max=most).astype(held_as)


def setup_inputs(seed: int = 0) -> dict:
    seeds = jax.random.split(jax.random.key(seed), 5)
    tokens = draw_tokens(jax.random.fold_in(seeds[4], 71), 0)
    w_qkv = scatter_about(seeds[1], (D, 3 * D), D ** -0.5, 0.1875, ((0, 32),))
    w_out = scatter_about(seeds[2], (D, D), D ** -0.5, 0.1875, ((0, 32),))
    neighbours = draw_neighbours(jax.random.fold_in(seeds[4], 71), 0)
    return dict(tokens=tokens, w_qkv=w_qkv, w_out=w_out, neighbours=neighbours)


def reference(tokens, w_qkv, w_out, neighbours):
    planes = tokens.reshape(NBLK // PB, PB * BLK, D)

    def project(rows):
        return jnp.dot(rows, w_qkv, preferred_element_type=jnp.float32).astype(jnp.bfloat16)
    qkv = lax.map(project, planes).reshape(NBLK, BLK, 3, HEADS, HD)
    qkv = jnp.transpose(qkv, (3, 2, 0, 1, 4))
    scale = 1.0 / math.sqrt(HD)
    lists = neighbours.reshape(NBLK // PB, PB, NBR)

    def one_head(parts):
        queries = parts[0].reshape(NBLK // PB, PB, BLK, HD)
        key_blocks = parts[1]
        value_blocks = parts[2]

        def one_plane(args):
            query_group, list_group = args
            keys = key_blocks[list_group].reshape(PB, NBR * BLK, HD)
            values = value_blocks[list_group].reshape(PB, NBR * BLK, HD)
            scores = jnp.einsum('nqd,nkd->nqk', query_group.astype(jnp.float32), keys.astype(jnp.float32)) * scale
            largest = lax.optimization_barrier(jnp.max(scores, axis=-1, keepdims=True))
            expo = jnp.exp(scores - largest)
            probs = (expo / lax.optimization_barrier(jnp.sum(expo, axis=-1, keepdims=True))).astype(jnp.bfloat16)
            return jnp.einsum('nqk,nkd->nqd', probs.astype(jnp.float32), values.astype(jnp.float32)).astype(jnp.bfloat16)
        return lax.map(one_plane, (queries, lists))
    attended = lax.map(one_head, qkv)
    attended = attended.reshape(HEADS, TOKENS, HD).transpose(1, 0, 2).reshape(TOKENS, D)
    return jnp.dot(attended, w_out, preferred_element_type=jnp.float32).astype(jnp.bfloat16)
```

```python
import functools
import math

import jax
import jax.numpy as jnp
from jax import lax
from jax.experimental import pallas as pl
from jax.experimental.pallas import tpu as pltpu
from jax.sharding import PartitionSpec as P

HEADS = 8
HD = 128
BLK = 128
NBR = 12
ROWS = 512
D = 1024
CHUNKS = 4
SLOTS = 9
SCALE = 1.0 / math.sqrt(HD)
MESH = pl.DeviceIdType.MESH


def gather_kernel(tok_ref, out_ref, local_sem, send_sem, recv_sem):
    seq = lax.axis_index("seq")
    head = lax.axis_index("head")
    seqs = 32
    x = head // 2
    zh = head % 2
    up = x // 2

    def at_x(bit):
        low = x % 2
        high = x // 2
        if bit & 1:
            low = 1 - low
        if bit & 2:
            high = 1 - high
        return {"seq": seq, "head": (high * 2 + low) * 2 + zh}

    step = 1 - 2 * up
    dev_z = {"seq": seq, "head": x * 2 + (1 - zh)}
    dev_1, dev_2, dev_3 = at_x(1), at_x(2), at_x(3)
    far_to = {"seq": lax.rem(seq + step + seqs, seqs), "head": head}
    far_from = {"seq": lax.rem(seq - step + seqs, seqs), "head": head}

    barrier = pltpu.get_barrier_semaphore()
    partners = (dev_z, dev_1, dev_2, dev_3, far_to, far_from)
    for dev in partners:
        pl.semaphore_signal(barrier, inc=1, device_id=dev, device_id_type=MESH)
    pl.semaphore_wait(barrier, len(partners))

    size = ROWS // CHUNKS

    def copy(kind, c, src, slot, dev):
        rows = pl.ds(c * size, size)
        return pltpu.make_async_remote_copy(
            src_ref=src.at[rows], dst_ref=out_ref.at[slot, rows],
            send_sem=send_sem.at[kind, c], recv_sem=recv_sem.at[kind, c],
            device_id=dev, device_id_type=MESH,
        )

    kinds = {
        0: (tok_ref, 1, dev_z),
        1: (tok_ref, 3, dev_2),
        2: (out_ref.at[1], 2, dev_1),
        3: (out_ref.at[1], 5, dev_3),
        4: (out_ref.at[2], 4, dev_3),
        5: (out_ref.at[5], 4, dev_1),
        6: (out_ref.at[3], 6, far_to),
        7: (out_ref.at[4], 7, far_to),
        8: (out_ref.at[5], 8, far_to),
    }
    made = {}

    def start(kind, c):
        src, slot, dev = kinds[kind]
        cp = copy(kind, c, src, slot, dev)
        cp.start()
        made[kind, c] = cp

    own = pltpu.make_async_copy(tok_ref, out_ref.at[0], local_sem)
    for c in range(CHUNKS):
        start(0, c)
    for c in range(CHUNKS):
        start(1, c)
    own.start()

    def middle(c):
        return 4 if c % 2 == 0 else 5

    for i in range(CHUNKS + 2):
        if i < CHUNKS:
            made[0, i].wait_recv()
            start(2, i)
            start(3, i)
            made[1, i].wait_recv()
            start(6, i)
        c = i - 1
        if 0 <= c < CHUNKS:
            made[2, c].wait_recv()
            made[3, c].wait_recv()
            start(middle(c), c)
            start(8, c)
        c = i - 2
        if 0 <= c < CHUNKS:
            made[middle(c), c].wait_recv()
            start(7, c)
    for c in range(CHUNKS):
        for kind in (6, 7, 8):
            made[kind, c].wait_recv()
    for cp in made.values():
        cp.wait_send()
    own.wait()


def gather_tokens(tokens):
    return pl.pallas_call(
        gather_kernel,
        out_shape=jax.ShapeDtypeStruct((SLOTS, ROWS, D), jnp.bfloat16),
        in_specs=[pl.BlockSpec(memory_space=pl.ANY)],
        out_specs=pl.BlockSpec(memory_space=pl.ANY),
        scratch_shapes=[
            pltpu.SemaphoreType.DMA,
            pltpu.SemaphoreType.DMA((9, CHUNKS)),
            pltpu.SemaphoreType.DMA((9, CHUNKS)),
        ],
        compiler_params=pltpu.CompilerParams(collective_id=0, has_side_effects=True),
        cost_estimate=pl.CostEstimate(flops=0, bytes_accessed=200 << 20, transcendentals=0),
        name="gather_tokens",
    )(tokens)


def attend_kernel(idx_ref, q_ref, k_ref, v_ref, w_ref, out_ref, att_ref):
    head = pl.program_id(0)
    for b in range(ROWS // BLK):
        q = q_ref[pl.ds(b * BLK, BLK), :]
        picks = [pl.multiple_of(idx_ref[b, j] * BLK, BLK) for j in range(NBR)]
        keys = jnp.concatenate([k_ref[pl.ds(i, BLK), :] for i in picks], axis=0)
        values = jnp.concatenate([v_ref[pl.ds(i, BLK), :] for i in picks], axis=0)
        scores = lax.dot_general(
            q, keys, (((1,), (1,)), ((), ())), preferred_element_type=jnp.float32
        ) * SCALE
        largest = jnp.max(scores, axis=-1, keepdims=True)
        expo = jnp.exp(scores - largest)
        total = jnp.sum(expo, axis=-1, keepdims=True)
        probs = (expo / total).astype(jnp.bfloat16)
        result = jnp.dot(probs, values, preferred_element_type=jnp.float32)
        att_ref[pl.ds(b * BLK, BLK), pl.ds(pl.multiple_of(head * HD, HD), HD)] = result.astype(jnp.bfloat16)

    @pl.when(head == HEADS - 1)
    def _():
        out_ref[...] = jnp.dot(
            att_ref[...], w_ref[...], preferred_element_type=jnp.float32
        ).astype(jnp.bfloat16)


def attend(idx, q, kv, w_out):
    total = SLOTS * ROWS
    return pl.pallas_call(
        attend_kernel,
        out_shape=jax.ShapeDtypeStruct((ROWS, D), jnp.bfloat16),
        grid_spec=pltpu.PrefetchScalarGridSpec(
            num_scalar_prefetch=1,
            grid=(HEADS,),
            in_specs=[
                pl.BlockSpec((ROWS, HD), lambda h, i: (0, h)),
                pl.BlockSpec((total, HD), lambda h, i: (0, h)),
                pl.BlockSpec((total, HD), lambda h, i: (0, HEADS + h)),
                pl.BlockSpec((D, D), lambda h, i: (0, 0)),
            ],
            out_specs=pl.BlockSpec((ROWS, D), lambda h, i: (0, 0)),
            scratch_shapes=[pltpu.VMEM((ROWS, D), jnp.bfloat16)],
        ),
        compiler_params=pltpu.CompilerParams(vmem_limit_bytes=40 << 20),
        name="attend",
    )(idx, q, kv, kv, w_out)


def local_lists(neighbours):
    seq = lax.axis_index("seq")
    head = lax.axis_index("head")
    rows = ROWS // BLK
    lists = lax.dynamic_slice_in_dim(neighbours, head * rows, rows, axis=0)
    up = head // 4
    plane = seq * 2 + up
    row = head % 4
    depth = 64
    step = jnp.mod(lists // 16 - plane, depth)
    near = jnp.where(up == 0, 1, depth - 1)
    kind = jnp.where(step == 0, 0, jnp.where(step == near, 1, 2))
    y = (lists // 4) % 4
    pair = row + 1 - 2 * (row % 2)
    which = jnp.where(y == row, 0, jnp.where(y == pair, 1, 2))
    return ((kind * 3 + which) * 4 + lists % 4).astype(jnp.int32)


def local(tokens, w_qkv, w_out, neighbours):
    full_qkv = lax.all_gather(w_qkv, "seq", axis=0, tiled=True)
    full_out = lax.all_gather(w_out, "seq", axis=0, tiled=True)
    idx = local_lists(neighbours)
    gathered = gather_tokens(tokens).reshape(SLOTS * ROWS, D)
    q = jnp.dot(tokens, full_qkv[:, :D], preferred_element_type=jnp.float32).astype(jnp.bfloat16)
    kv = jnp.dot(gathered, full_qkv[:, D:], preferred_element_type=jnp.float32).astype(jnp.bfloat16)
    return attend(idx, q, kv, full_out)


def solution(mesh):
    return jax.shard_map(
        local,
        mesh=mesh,
        in_specs=(P(("seq", "head"), None), P("seq", None), P("seq", None), P("seq", None)),
        out_specs=P(("seq", "head"), None),
        check_vma=False,
    )
```

```python
import math

import jax
import jax.numpy as jnp
from jax import lax
from jax.experimental import pallas as pl
from jax.experimental.pallas import tpu as pltpu
from jax.sharding import PartitionSpec as P

HEADS = 8
HD = 128
BLK = 128
NBR = 12
ROWS = 512
D = 1024
SLOTS = 9
FACTOR = math.log2(math.e) / math.sqrt(HD)
MESH = pl.DeviceIdType.MESH
CHUNKS = 8
SIZE = ROWS // CHUNKS
PIECES = 4
PIECE = ROWS // PIECES
TICKS = CHUNKS + 2
OWN, PAIR, THIRD = 0, 1, 2
NEAR, FAR = 3, 6


def layer_kernel(idx_ref, tok_ref, wqkv_ref, wout_ref, out_ref,
                 toks, wkv, wqo, kv, qs, att,
                 tsend, trecv, wsend, wrecv):
    seq = lax.axis_index("seq")
    head = lax.axis_index("head")
    y = seq // 8
    zl = (seq // 2) % 4
    core = seq % 2
    x = head // 2
    zh = head % 2
    z = zh * 4 + zl
    up = x // 2

    def device(dx=0, dy=0, dz=0, dc=0):
        nz = lax.rem(z + dz + 8, 8)
        ny = lax.rem(y + dy + 4, 4)
        nx = lax.rem(x + dx + 4, 4)
        nc = lax.rem(core + dc, 2)
        return {"seq": ny * 8 + lax.rem(nz, 4) * 2 + nc, "head": nx * 2 + nz // 4}

    def at_x(low, high):
        nl = lax.rem(x % 2 + low, 2)
        nh = lax.rem(up + high, 2)
        return {"seq": seq, "head": (nh * 2 + nl) * 2 + zh}

    step = 1 - 2 * up
    dev_z = device(dz=4)
    dev_1, dev_2, dev_3 = at_x(1, 0), at_x(0, 1), at_x(1, 1)
    far_to = {"seq": lax.rem(seq + step + 32, 32), "head": head}
    far_from = {"seq": lax.rem(seq - step + 32, 32), "head": head}
    w_z = (device(dz=1), device(dz=-1), device(dz=2))
    w_z_from = (device(dz=-1), device(dz=1), device(dz=-2))
    w_x = (device(dx=1), device(dx=-1), device(dx=2))
    w_y = (device(dy=1), device(dy=-1))
    sibling = device(dc=1)

    barrier = pltpu.get_barrier_semaphore()
    partners = (dev_z, dev_1, dev_2, dev_3, far_to, far_from) + w_z + w_z_from + w_x + w_y + (sibling,)
    for dev in partners:
        pl.semaphore_signal(barrier, inc=1, device_id=dev, device_id_type=MESH)

    wkv[y, zl, core] = wqkv_ref[:, D:]
    wqo[y, zl, core, :, :D] = wqkv_ref[:, :D]
    wqo[y, zl, core, :, D:] = wout_ref[...]
    toks[pl.ds(0, ROWS)] = tok_ref[...]
    pl.semaphore_wait(barrier, len(partners))

    weights = (wkv, wqo)
    quarter = pl.ds(pl.multiple_of(x * 512, 512), 512)
    made_w = {}

    def send_w(g, number, where, dev):
        cp = pltpu.make_async_remote_copy(
            src_ref=weights[g].at[where], dst_ref=weights[g].at[where],
            send_sem=wsend.at[g, number], recv_sem=wrecv.at[g, number],
            device_id=dev, device_id_type=MESH,
        )
        cp.start()
        made_w[g, number] = cp

    def got_w(g, *numbers):
        for number in numbers:
            made_w[g, number].wait_recv()

    every = slice(None)

    def w_stage_z(g):
        for j in range(3):
            send_w(g, j, (y, zl, core, every, quarter), w_z[j])

    def w_stage_x(g):
        for j, dz in enumerate((3, 1, 2)):
            got_w(g, j)
            for i in range(3):
                send_w(g, 3 + 3 * j + i, (y, lax.rem(zl + dz, 4), core, every, quarter), w_x[i])

    def w_stage_y(g):
        got_w(g, *range(3, 12))
        send_w(g, 12, (y, every, core), w_y[0])
        send_w(g, 13, (y, every, core), w_y[1])
        send_w(g, 16, (y, every, core), sibling)

    def w_stage_relay(g):
        down = lax.rem(y + 3, 4)
        above = lax.rem(y + 1, 4)
        got_w(g, 12)
        send_w(g, 14, (down, pl.ds(0, 2), core), w_y[0])
        send_w(g, 17, (down, every, core), sibling)
        got_w(g, 13)
        send_w(g, 15, (above, pl.ds(2, 2), core), w_y[1])
        send_w(g, 18, (above, every, core), sibling)

    def w_stage_last(g):
        across = lax.rem(y + 2, 4)
        got_w(g, 14)
        send_w(g, 19, (across, pl.ds(0, 2), core), sibling)
        got_w(g, 15)
        send_w(g, 20, (across, pl.ds(2, 2), core), sibling)

    def w_ready(g):
        got_w(g, *range(16, 21))

    kinds = {
        0: (OWN, PAIR, dev_z),
        1: (OWN, NEAR + OWN, dev_2),
        2: (PAIR, THIRD, dev_1),
        3: (PAIR, NEAR + THIRD, dev_3),
        4: (THIRD, NEAR + PAIR, dev_3),
        5: (NEAR + THIRD, NEAR + PAIR, dev_1),
        6: (NEAR + OWN, FAR + OWN, far_to),
        7: (NEAR + PAIR, FAR + PAIR, far_to),
        8: (NEAR + THIRD, FAR + THIRD, far_to),
    }
    made = {}

    def send(kind, c):
        src, dst, dev = kinds[kind]
        cp = pltpu.make_async_remote_copy(
            src_ref=toks.at[pl.ds(src * ROWS + c * SIZE, SIZE)],
            dst_ref=toks.at[pl.ds(dst * ROWS + c * SIZE, SIZE)],
            send_sem=tsend.at[kind, c], recv_sem=trecv.at[kind, c],
            device_id=dev, device_id_type=MESH,
        )
        cp.start()
        made[kind, c] = cp

    def middle(c):
        return 4 if c % 2 == 0 else 5

    def tick(i):
        if i < CHUNKS:
            made[0, i].wait_recv()
            send(2, i)
            send(3, i)
            made[1, i].wait_recv()
            send(6, i)
        c = i - 1
        if 0 <= c < CHUNKS:
            made[2, c].wait_recv()
            made[3, c].wait_recv()
            send(middle(c), c)
            send(8, c)
        c = i - 2
        if 0 <= c < CHUNKS:
            made[middle(c), c].wait_recv()
            send(7, c)

    per = CHUNKS // PIECES
    ready = {}
    for p in range(PIECES):
        last = per * (p + 1) - 1
        ready[OWN, p] = 0
        ready[PAIR, p] = last
        ready[NEAR + OWN, p] = last
        ready[THIRD, p] = last + 1
        ready[NEAR + THIRD, p] = last + 1
        ready[NEAR + PAIR, p] = last + 2
        ready[FAR + OWN, p] = last + 2
        ready[FAR + THIRD, p] = last + 3
        ready[FAR + PAIR, p] = last + 4
    pending = sorted(ready, key=lambda k: (ready[k], k))
    far_kind = {FAR + OWN: 6, FAR + PAIR: 7, FAR + THIRD: 8}

    def project(keys):
        offsets = []
        for slot, p in keys:
            if slot >= FAR:
                for c in range(per * p, per * (p + 1)):
                    made[far_kind[slot], c].wait_recv()
            offsets.append(slot * PIECES + p)

        def body(k, carry):
            n = k % 2
            which = k // 2
            row = jnp.int32(offsets[0])
            for j in range(1, len(offsets)):
                row = jnp.where(which == j, offsets[j], row)
            rows = pl.ds(pl.multiple_of(row * PIECE, PIECE), PIECE)
            cols = pl.ds(pl.multiple_of(n * D, D), D)
            w = wkv[:, :, :, :, cols].reshape(D, D)
            kv[row, :, cols] = jnp.dot(
                toks[rows, :], w, preferred_element_type=jnp.float32
            ).astype(jnp.bfloat16)
            return carry

        lax.fori_loop(0, 2 * len(offsets), body, 0)

    def project_up_to(t, limit):
        keys = [k for k in pending if ready[k] <= t][:limit]
        for k in keys:
            pending.remove(k)
        if keys:
            project(keys)

    w_stage_z(0)
    for c in range(CHUNKS):
        send(0, c)
    w_stage_z(1)
    w_stage_x(0)
    for c in range(CHUNKS):
        send(1, c)
    w_stage_y(0)
    tick(0)
    w_stage_x(1)
    tick(1)
    w_stage_relay(0)
    w_stage_y(1)
    tick(2)
    w_stage_last(0)
    tick(3)
    w_ready(0)
    project_up_to(3, 8)
    tick(4)
    project_up_to(4, 8)
    w_stage_relay(1)
    tick(5)
    project_up_to(5, 8)
    w_stage_last(1)
    tick(6)
    project_up_to(6, 8)
    w_ready(1)

    def q_body(n, carry):
        cols = pl.ds(pl.multiple_of(n * 512, 512), 512)
        w = wqo[:, :, :, :, cols].reshape(D, 512)
        qs[:, cols] = jnp.dot(
            toks[pl.ds(0, ROWS), :], w, preferred_element_type=jnp.float32
        ).astype(jnp.bfloat16)
        return carry

    lax.fori_loop(0, 2, q_body, 0)
    tick(7)
    project_up_to(7, 8)
    tick(8)
    project_up_to(8, 8)
    tick(9)
    project_up_to(9, 36)
    project_up_to(10, 36)
    project_up_to(11, 36)

    def one_head(h, carry):
        key_cols = pl.ds(pl.multiple_of(h * HD, HD), HD)
        value_cols = pl.ds(pl.multiple_of(h * HD + D, HD), HD)
        for b in range(ROWS // BLK):
            q = qs[pl.ds(b * BLK, BLK), key_cols]
            picks = [idx_ref[b, j] for j in range(NBR)]
            keys = jnp.concatenate([kv[i, :, key_cols] for i in picks], axis=0)
            values = jnp.concatenate([kv[i, :, value_cols] for i in picks], axis=0)
            scores = lax.dot_general(
                q, keys, (((1,), (1,)), ((), ())), preferred_element_type=jnp.float32
            )
            largest = jnp.max(scores, axis=-1, keepdims=True) * FACTOR
            expo = jnp.exp2(scores * FACTOR - largest)
            total = jnp.sum(expo, axis=-1, keepdims=True)
            result = jnp.dot(expo.astype(jnp.bfloat16), values, preferred_element_type=jnp.float32)
            att[pl.ds(b * BLK, BLK), key_cols] = (result * (1.0 / total)).astype(jnp.bfloat16)
        return carry

    lax.fori_loop(0, HEADS, one_head, 0)

    def out_body(n, carry):
        cols = pl.ds(pl.multiple_of(n * 512, 512), 512)
        w = wqo[:, :, :, :, pl.ds(pl.multiple_of(D + n * 512, 512), 512)].reshape(D, 512)
        out_ref[:, cols] = jnp.dot(
            att[...], w, preferred_element_type=jnp.float32
        ).astype(jnp.bfloat16)
        return carry

    lax.fori_loop(0, 2, out_body, 0)
    for cp in made.values():
        cp.wait_send()
    for cp in made_w.values():
        cp.wait_send()


def layer(idx, tokens, w_qkv, w_out):
    vmem = pl.BlockSpec(memory_space=pltpu.VMEM)
    bf16 = jnp.bfloat16
    return pl.pallas_call(
        layer_kernel,
        out_shape=jax.ShapeDtypeStruct((ROWS, D), bf16),
        in_specs=[pl.BlockSpec(memory_space=pltpu.SMEM), vmem, vmem, vmem],
        out_specs=vmem,
        scratch_shapes=[
            pltpu.VMEM((SLOTS * ROWS, D), bf16),
            pltpu.VMEM((4, 4, 2, 32, 2 * D), bf16),
            pltpu.VMEM((4, 4, 2, 32, 2 * D), bf16),
            pltpu.VMEM((SLOTS * ROWS // BLK, BLK, 2 * D), bf16),
            pltpu.VMEM((ROWS, D), bf16),
            pltpu.VMEM((ROWS, D), bf16),
            pltpu.SemaphoreType.DMA((9, CHUNKS)),
            pltpu.SemaphoreType.DMA((9, CHUNKS)),
            pltpu.SemaphoreType.DMA((2, 21)),
            pltpu.SemaphoreType.DMA((2, 21)),
        ],
        compiler_params=pltpu.CompilerParams(
            collective_id=0, has_side_effects=True, vmem_limit_bytes=56 << 20
        ),
        name="layer",
    )(idx, tokens, w_qkv, w_out)


def local_lists(neighbours):
    seq = lax.axis_index("seq")
    head = lax.axis_index("head")
    rows = ROWS // BLK
    lists = lax.dynamic_slice_in_dim(neighbours, head * rows, rows, axis=0)
    up = head // 4
    plane = seq * 2 + up
    row = head % 4
    depth = 64
    step = jnp.mod(lists // 16 - plane, depth)
    near = jnp.where(up == 0, 1, depth - 1)
    kind = jnp.where(step == 0, 0, jnp.where(step == near, 1, 2))
    y = (lists // 4) % 4
    pair = row + 1 - 2 * (row % 2)
    which = jnp.where(y == row, 0, jnp.where(y == pair, 1, 2))
    return ((kind * 3 + which) * 4 + lists % 4).astype(jnp.int32)


def local(tokens, w_qkv, w_out, neighbours):
    return layer(local_lists(neighbours), tokens, w_qkv, w_out)


def solution(mesh):
    return jax.shard_map(
        local,
        mesh=mesh,
        in_specs=(P(("seq", "head"), None), P("seq", None), P("seq", None), P("seq", None)),
        out_specs=P(("seq", "head"), None),
        check_vma=False,
    )
```

```python
import math

import jax
import jax.numpy as jnp
from jax import lax
from jax.experimental import pallas as pl
from jax.experimental.pallas import tpu as pltpu
from jax.sharding import PartitionSpec as P

HEADS = 8
HD = 128
BLK = 128
NBR = 12
ROWS = 512
D = 1024
SLOTS = 9
FACTOR = math.log2(math.e) / math.sqrt(HD)
MESH = pl.DeviceIdType.MESH
CHUNKS = 8
SIZE = ROWS // CHUNKS
PIECES = 4
PIECE = ROWS // PIECES
AHEAD = 3
NEAR_AHEAD = 2
RELAYED = (1, 4, 6)
OWN, PAIR, THIRD = 0, 1, 2
NEAR, FAR = 3, 6


def layer_kernel(idx_ref, tok_ref, wqkv_ref, wout_ref, out_ref,
                 toks, wkv, wqo, kv, qs, att,
                 relayed, tsend, trecv, wsend, wrecv):
    seq = lax.axis_index("seq")
    head = lax.axis_index("head")
    y = seq // 8
    zl = (seq // 2) % 4
    core = seq % 2
    x = head // 2
    zh = head % 2
    z = zh * 4 + zl
    up = x // 2

    def device(dx=0, dy=0, dz=0, dc=0):
        nz = lax.rem(z + dz + 8, 8)
        ny = lax.rem(y + dy + 4, 4)
        nx = lax.rem(x + dx + 4, 4)
        nc = lax.rem(core + dc, 2)
        return {"seq": ny * 8 + lax.rem(nz, 4) * 2 + nc, "head": nx * 2 + nz // 4}

    def at_x(low, high):
        nl = lax.rem(x % 2 + low, 2)
        nh = lax.rem(up + high, 2)
        return {"seq": seq, "head": (nh * 2 + nl) * 2 + zh}

    step = 1 - 2 * up
    dev_z = device(dz=4)
    dev_1, dev_2, dev_3 = at_x(1, 0), at_x(0, 1), at_x(1, 1)
    end = lax.rem(seq, 8)
    cross_to = jnp.where(end == 7 * (1 - up), 1, 0)
    cross_from = jnp.where(end == 7 * up, 1, 0)
    seq_to = lax.rem(seq + step + 32, 32)
    seq_from = lax.rem(seq - step + 32, 32)

    def across(seq_at, low, turn):
        return {"seq": seq_at, "head": (up * 2 + lax.rem(x % 2 + low, 2)) * 2 + lax.rem(zh + turn, 2)}

    far_to = across(seq_to, 0, cross_to)
    far_to_third = across(seq_to, cross_to, cross_to)
    far_from = across(seq_from, 0, cross_from)
    far_from_third = across(seq_from, cross_from, cross_from)
    relay_to, relay_from = device(dz=-step), device(dz=step)
    onward_to, onward_from = device(dz=-3 * step), device(dz=3 * step)
    w_z = (device(dz=1), device(dz=-1), device(dz=2))
    w_z_from = (device(dz=-1), device(dz=1), device(dz=-2))
    w_x = (device(dx=1), device(dx=-1), device(dx=2))
    w_y = (device(dy=1), device(dy=-1))
    sibling = device(dc=1)

    barrier = pltpu.get_barrier_semaphore()
    partners = (dev_z, dev_1, dev_2, dev_3, far_to, far_from, far_to_third, far_from_third)
    partners += (onward_to, onward_from) + w_z + w_z_from + w_x + w_y + (sibling,)
    for dev in partners:
        pl.semaphore_signal(barrier, inc=1, device_id=dev, device_id_type=MESH)

    wkv[y, zl, core] = wqkv_ref[:, D:]
    wqo[y, zl, core, :, :D] = wqkv_ref[:, :D]
    wqo[y, zl, core, :, D:] = wout_ref[...]
    toks[pl.ds(0, ROWS)] = tok_ref[...]
    pl.semaphore_wait(barrier, len(partners))

    weights = (wkv, wqo)
    quarter = pl.ds(pl.multiple_of(x * 512, 512), 512)
    made_w = {}

    def send_w(g, number, where, dev):
        cp = pltpu.make_async_remote_copy(
            src_ref=weights[g].at[where], dst_ref=weights[g].at[where],
            send_sem=wsend.at[g, number], recv_sem=wrecv.at[g, number],
            device_id=dev, device_id_type=MESH,
        )
        cp.start()
        made_w[g, number] = cp

    def got_w(g, *numbers):
        for number in numbers:
            made_w[g, number].wait_recv()

    every = slice(None)

    def w_stage_z(g):
        for j in range(3):
            send_w(g, j, (y, zl, core, every, quarter), w_z[j])

    def w_stage_x(g):
        for j, dz in enumerate((3, 1, 2)):
            got_w(g, j)
            for i in range(3):
                send_w(g, 3 + 3 * j + i, (y, lax.rem(zl + dz, 4), core, every, quarter), w_x[i])

    def w_stage_y(g):
        got_w(g, *range(3, 12))
        send_w(g, 12, (y, every, core), w_y[0])
        send_w(g, 13, (y, every, core), w_y[1])
        send_w(g, 16, (y, every, core), sibling)

    def w_stage_relay(g):
        down = lax.rem(y + 3, 4)
        above = lax.rem(y + 1, 4)
        got_w(g, 12)
        send_w(g, 14, (down, pl.ds(0, 2), core), w_y[0])
        send_w(g, 17, (down, every, core), sibling)
        got_w(g, 13)
        send_w(g, 15, (above, pl.ds(2, 2), core), w_y[1])
        send_w(g, 18, (above, every, core), sibling)

    def w_stage_last(g):
        across = lax.rem(y + 2, 4)
        got_w(g, 14)
        send_w(g, 19, (across, pl.ds(0, 2), core), sibling)
        got_w(g, 15)
        send_w(g, 20, (across, pl.ds(2, 2), core), sibling)

    def w_ready(g):
        got_w(g, *range(16, 21))

    kinds = {
        0: (OWN, PAIR, 0, dev_z),
        1: (OWN, NEAR + OWN, 1, dev_2),
        2: (PAIR, THIRD, 2, dev_1),
        3: (PAIR, NEAR + THIRD, 3, dev_3),
        4: (THIRD, NEAR + PAIR, 4, dev_3),
        5: (NEAR + THIRD, NEAR + PAIR, 4, dev_1),
        6: (NEAR + OWN, FAR + OWN + cross_to, 6 + cross_to, far_to),
        7: (NEAR + PAIR, FAR + PAIR - cross_to, 7 - cross_to, far_to),
        8: (NEAR + THIRD - 2 * cross_to, FAR + THIRD, 8, far_to_third),
    }
    made = []

    def rows_of(slot, c):
        return pl.ds(pl.multiple_of(slot * ROWS + c * SIZE, SIZE), SIZE)

    def move(src, dst, kind, wait_row, c, dev):
        cp = pltpu.make_async_remote_copy(
            src_ref=src, dst_ref=dst, send_sem=tsend.at[kind, c], recv_sem=trecv.at[wait_row, c],
            device_id=dev, device_id_type=MESH,
        )
        cp.start()
        made.append(cp)

    def send(kind, c):
        src, dst, wait_row, dev = kinds[kind]
        move(toks.at[rows_of(src, c)], toks.at[rows_of(dst, c)], kind, wait_row, c, dev)

    slot_of_row = (PAIR, NEAR + OWN, THIRD, NEAR + THIRD, NEAR + PAIR, None, FAR + OWN, FAR + PAIR, FAR + THIRD)

    def wait_in(ref, row, c):
        pltpu.make_async_remote_copy(
            src_ref=ref, dst_ref=ref, send_sem=tsend.at[row, c], recv_sem=trecv.at[row, c],
            device_id=dev_z, device_id_type=MESH,
        ).wait_recv()

    def arrived(row, c):
        wait_in(toks.at[rows_of(slot_of_row[row], c)], row, c)

    def send_pair(c):
        if c >= CHUNKS:
            return
        if c in RELAYED:
            move(toks.at[rows_of(OWN, c)], relayed.at[RELAYED.index(c)], 0, 9, c, relay_to)
        else:
            send(0, c)

    def pass_on(c):
        if c in RELAYED:
            buffer = relayed.at[RELAYED.index(c)]
            wait_in(buffer, 9, c)
            move(buffer, toks.at[rows_of(PAIR, c)], 9, 0, c, onward_to)

    def tick(i):
        if i < CHUNKS:
            pass_on(i + 2)
            arrived(0, i)
            send_pair(i + AHEAD)
            send(2, i)
            send(3, i)
            arrived(1, i)
            if i + NEAR_AHEAD < CHUNKS:
                send(1, i + NEAR_AHEAD)
            send(6, i)
        c = i - 1
        if 0 <= c < CHUNKS:
            arrived(2, c)
            arrived(3, c)
            send(4 if c % 2 == 0 else 5, c)
            send(8, c)
        c = i - 2
        if 0 <= c < CHUNKS:
            arrived(4, c)
            send(7, c)

    per = CHUNKS // PIECES
    ready = {}
    for p in range(PIECES):
        last = per * (p + 1) - 1
        ready[OWN, p] = 0
        ready[PAIR, p] = last
        ready[NEAR + OWN, p] = last
        ready[THIRD, p] = last + 1
        ready[NEAR + THIRD, p] = last + 1
        ready[NEAR + PAIR, p] = last + 2
        ready[FAR + OWN, p] = last + 4
        ready[FAR + THIRD, p] = last + 3
        ready[FAR + PAIR, p] = last + 4
    pending = sorted(ready, key=lambda k: (ready[k], k))

    def project(keys):
        offsets = []
        for slot, p in keys:
            if slot >= FAR:
                for c in range(per * p, per * (p + 1)):
                    arrived(slot, c)
            offsets.append(slot * PIECES + p)

        def body(k, carry):
            n = k % 2
            which = k // 2
            row = jnp.int32(offsets[0])
            for j in range(1, len(offsets)):
                row = jnp.where(which == j, offsets[j], row)
            rows = pl.ds(pl.multiple_of(row * PIECE, PIECE), PIECE)
            cols = pl.ds(pl.multiple_of(n * D, D), D)
            w = wkv[:, :, :, :, cols].reshape(D, D)
            kv[row, :, cols] = jnp.dot(
                toks[rows, :], w, preferred_element_type=jnp.float32
            ).astype(jnp.bfloat16)
            return carry

        lax.fori_loop(0, 2 * len(offsets), body, 0)

    def project_up_to(t, limit):
        keys = [k for k in pending if ready[k] <= t][:limit]
        for k in keys:
            pending.remove(k)
        if keys:
            project(keys)

    w_stage_z(0)
    for c in range(AHEAD):
        send_pair(c)
    w_stage_z(1)
    w_stage_x(0)
    for c in range(NEAR_AHEAD):
        send(1, c)
    pass_on(0)
    pass_on(1)
    w_stage_y(0)
    tick(0)
    w_stage_x(1)
    tick(1)
    w_stage_relay(0)
    w_stage_y(1)
    tick(2)
    w_stage_last(0)
    tick(3)
    w_ready(0)
    project_up_to(3, 8)
    tick(4)
    project_up_to(4, 8)
    w_stage_relay(1)
    tick(5)
    project_up_to(5, 8)
    w_stage_last(1)
    tick(6)
    project_up_to(6, 8)
    w_ready(1)

    def q_body(n, carry):
        cols = pl.ds(pl.multiple_of(n * 512, 512), 512)
        w = wqo[:, :, :, :, cols].reshape(D, 512)
        qs[:, cols] = jnp.dot(
            toks[pl.ds(0, ROWS), :], w, preferred_element_type=jnp.float32
        ).astype(jnp.bfloat16)
        return carry

    lax.fori_loop(0, 2, q_body, 0)
    tick(7)
    project_up_to(7, 8)
    tick(8)
    project_up_to(8, 8)
    tick(9)
    project_up_to(9, 36)
    project_up_to(10, 36)
    project_up_to(11, 36)

    def one_head(h, carry):
        key_cols = pl.ds(pl.multiple_of(h * HD, HD), HD)
        value_cols = pl.ds(pl.multiple_of(h * HD + D, HD), HD)
        for b in range(ROWS // BLK):
            q = qs[pl.ds(b * BLK, BLK), key_cols]
            picks = [idx_ref[b, j] for j in range(NBR)]
            keys = jnp.concatenate([kv[i, :, key_cols] for i in picks], axis=0)
            values = jnp.concatenate([kv[i, :, value_cols] for i in picks], axis=0)
            scores = lax.dot_general(
                q, keys, (((1,), (1,)), ((), ())), preferred_element_type=jnp.float32
            )
            largest = jnp.max(scores, axis=-1, keepdims=True) * FACTOR
            expo = jnp.exp2(scores * FACTOR - largest)
            total = jnp.sum(expo, axis=-1, keepdims=True)
            result = jnp.dot(expo.astype(jnp.bfloat16), values, preferred_element_type=jnp.float32)
            att[pl.ds(b * BLK, BLK), key_cols] = (result * (1.0 / total)).astype(jnp.bfloat16)
        return carry

    lax.fori_loop(0, HEADS, one_head, 0)

    def out_body(n, carry):
        cols = pl.ds(pl.multiple_of(n * 512, 512), 512)
        w = wqo[:, :, :, :, pl.ds(pl.multiple_of(D + n * 512, 512), 512)].reshape(D, 512)
        out_ref[:, cols] = jnp.dot(
            att[...], w, preferred_element_type=jnp.float32
        ).astype(jnp.bfloat16)
        return carry

    lax.fori_loop(0, 2, out_body, 0)
    for cp in made:
        cp.wait_send()
    for cp in made_w.values():
        cp.wait_send()


def layer(idx, tokens, w_qkv, w_out):
    vmem = pl.BlockSpec(memory_space=pltpu.VMEM)
    bf16 = jnp.bfloat16
    return pl.pallas_call(
        layer_kernel,
        out_shape=jax.ShapeDtypeStruct((ROWS, D), bf16),
        in_specs=[pl.BlockSpec(memory_space=pltpu.SMEM), vmem, vmem, vmem],
        out_specs=vmem,
        scratch_shapes=[
            pltpu.VMEM((SLOTS * ROWS, D), bf16),
            pltpu.VMEM((4, 4, 2, 32, 2 * D), bf16),
            pltpu.VMEM((4, 4, 2, 32, 2 * D), bf16),
            pltpu.VMEM((SLOTS * ROWS // BLK, BLK, 2 * D), bf16),
            pltpu.VMEM((ROWS, D), bf16),
            pltpu.VMEM((ROWS, D), bf16),
            pltpu.VMEM((len(RELAYED), SIZE, D), bf16),
            pltpu.SemaphoreType.DMA((10, CHUNKS)),
            pltpu.SemaphoreType.DMA((10, CHUNKS)),
            pltpu.SemaphoreType.DMA((2, 21)),
            pltpu.SemaphoreType.DMA((2, 21)),
        ],
        compiler_params=pltpu.CompilerParams(
            collective_id=0, has_side_effects=True, vmem_limit_bytes=56 << 20
        ),
        name="layer",
    )(idx, tokens, w_qkv, w_out)


def local_lists(neighbours):
    seq = lax.axis_index("seq")
    head = lax.axis_index("head")
    rows = ROWS // BLK
    lists = lax.dynamic_slice_in_dim(neighbours, head * rows, rows, axis=0)
    up = head // 4
    plane = seq * 2 + up
    row = head % 4
    depth = 64
    step = jnp.mod(lists // 16 - plane, depth)
    near = jnp.where(up == 0, 1, depth - 1)
    kind = jnp.where(step == 0, 0, jnp.where(step == near, 1, 2))
    y = (lists // 4) % 4
    pair = row + 1 - 2 * (row % 2)
    which = jnp.where(y == row, 0, jnp.where(y == pair, 1, 2))
    return ((kind * 3 + which) * 4 + lists % 4).astype(jnp.int32)


def local(tokens, w_qkv, w_out, neighbours):
    return layer(local_lists(neighbours), tokens, w_qkv, w_out)


def solution(mesh):
    return jax.shard_map(
        local,
        mesh=mesh,
        in_specs=(P(("seq", "head"), None), P("seq", None), P("seq", None), P("seq", None)),
        out_specs=P(("seq", "head"), None),
        check_vma=False,
    )
```

```python
import math

import jax
import jax.numpy as jnp
from jax import lax
from jax.experimental import pallas as pl
from jax.experimental.pallas import tpu as pltpu
from jax.sharding import PartitionSpec as P

HEADS = 8
HD = 128
BLK = 128
NBR = 12
ROWS = 512
D = 1024
SLOTS = 9
FACTOR = math.log2(math.e) / math.sqrt(HD)
MESH = pl.DeviceIdType.MESH
CHUNKS = 8
SIZE = ROWS // CHUNKS
PIECES = 4
PIECE = ROWS // PIECES
AHEAD = 3
NEAR_AHEAD = 3
RELAYED = (1, 4, 6)
OWN, PAIR, THIRD = 0, 1, 2
NEAR, FAR = 3, 6


def layer_kernel(idx_ref, tok_ref, wqkv_ref, wout_ref, out_ref,
                 toks, wkv, wqo, kv, qs, att,
                 relayed, tsend, trecv, wsend, wrecv):
    seq = lax.axis_index("seq")
    head = lax.axis_index("head")
    y = seq // 8
    zl = (seq // 2) % 4
    core = seq % 2
    x = head // 2
    zh = head % 2
    z = zh * 4 + zl
    up = x // 2

    def device(dx=0, dy=0, dz=0, dc=0):
        nz = lax.rem(z + dz + 8, 8)
        ny = lax.rem(y + dy + 4, 4)
        nx = lax.rem(x + dx + 4, 4)
        nc = lax.rem(core + dc, 2)
        return {"seq": ny * 8 + lax.rem(nz, 4) * 2 + nc, "head": nx * 2 + nz // 4}

    def at_x(low, high):
        nl = lax.rem(x % 2 + low, 2)
        nh = lax.rem(up + high, 2)
        return {"seq": seq, "head": (nh * 2 + nl) * 2 + zh}

    step = 1 - 2 * up
    dev_z = device(dz=4)
    dev_1, dev_2, dev_3 = at_x(1, 0), at_x(0, 1), at_x(1, 1)
    end = lax.rem(seq, 8)
    cross_to = jnp.where(end == 7 * (1 - up), 1, 0)
    cross_from = jnp.where(end == 7 * up, 1, 0)
    seq_to = lax.rem(seq + step + 32, 32)
    seq_from = lax.rem(seq - step + 32, 32)

    def across(seq_at, low, turn):
        return {"seq": seq_at, "head": (up * 2 + lax.rem(x % 2 + low, 2)) * 2 + lax.rem(zh + turn, 2)}

    far_to = across(seq_to, 0, cross_to)
    far_to_third = across(seq_to, cross_to, cross_to)
    far_from = across(seq_from, 0, cross_from)
    far_from_third = across(seq_from, cross_from, cross_from)
    relay_to, relay_from = device(dz=-step), device(dz=step)
    onward_to, onward_from = device(dz=-3 * step), device(dz=3 * step)
    w_z = (device(dz=1), device(dz=-1), device(dz=2))
    w_z_from = (device(dz=-1), device(dz=1), device(dz=-2))
    w_x = (device(dx=1), device(dx=-1), device(dx=2))
    w_y = (device(dy=1), device(dy=-1))
    sibling = device(dc=1)

    barrier = pltpu.get_barrier_semaphore()
    partners = (dev_z, dev_1, dev_2, dev_3, far_to, far_from, far_to_third, far_from_third)
    partners += (onward_to, onward_from) + w_z + w_z_from + w_x + w_y + (sibling,)
    for dev in partners:
        pl.semaphore_signal(barrier, inc=1, device_id=dev, device_id_type=MESH)

    wkv[y, zl, core] = wqkv_ref[:, D:]
    wqo[y, zl, core, :, :D] = wqkv_ref[:, :D]
    wqo[y, zl, core, :, D:] = wout_ref[...]
    toks[pl.ds(0, ROWS)] = tok_ref[...]
    pl.semaphore_wait(barrier, len(partners))

    weights = (wkv, wqo)
    quarter = pl.ds(pl.multiple_of(x * 512, 512), 512)
    made_w = {}

    def send_w(g, number, where, dev):
        cp = pltpu.make_async_remote_copy(
            src_ref=weights[g].at[where], dst_ref=weights[g].at[where],
            send_sem=wsend.at[g, number], recv_sem=wrecv.at[g, number],
            device_id=dev, device_id_type=MESH,
        )
        cp.start()
        made_w[g, number] = cp

    def got_w(g, *numbers):
        for number in numbers:
            made_w[g, number].wait_recv()

    every = slice(None)

    def w_stage_z(g):
        for j in range(3):
            send_w(g, j, (y, zl, core, every, quarter), w_z[j])

    def w_stage_x(g):
        for j, dz in enumerate((3, 1, 2)):
            got_w(g, j)
            for i in range(3):
                send_w(g, 3 + 3 * j + i, (y, lax.rem(zl + dz, 4), core, every, quarter), w_x[i])

    def w_stage_y(g):
        got_w(g, *range(3, 12))
        send_w(g, 12, (y, every, core), w_y[0])
        send_w(g, 13, (y, every, core), w_y[1])
        send_w(g, 16, (y, every, core), sibling)

    def w_stage_relay(g):
        down = lax.rem(y + 3, 4)
        above = lax.rem(y + 1, 4)
        got_w(g, 12)
        send_w(g, 14, (down, pl.ds(0, 2), core), w_y[0])
        send_w(g, 17, (down, every, core), sibling)
        got_w(g, 13)
        send_w(g, 15, (above, pl.ds(2, 2), core), w_y[1])
        send_w(g, 18, (above, every, core), sibling)

    def w_stage_last(g):
        across = lax.rem(y + 2, 4)
        got_w(g, 14)
        send_w(g, 19, (across, pl.ds(0, 2), core), sibling)
        got_w(g, 15)
        send_w(g, 20, (across, pl.ds(2, 2), core), sibling)

    def w_ready(g):
        got_w(g, *range(16, 21))

    kinds = {
        0: (OWN, PAIR, 0, dev_z),
        1: (OWN, NEAR + OWN, 1, dev_2),
        2: (PAIR, THIRD, 2, dev_1),
        3: (PAIR, NEAR + THIRD, 3, dev_3),
        4: (THIRD, NEAR + PAIR, 4, dev_3),
        5: (NEAR + THIRD, NEAR + PAIR, 4, dev_1),
        6: (NEAR + OWN, FAR + OWN + cross_to, 6 + cross_to, far_to),
        7: (NEAR + PAIR, FAR + PAIR - cross_to, 7 - cross_to, far_to),
        8: (NEAR + THIRD - 2 * cross_to, FAR + THIRD, 8, far_to_third),
    }
    made = []

    def rows_of(slot, c):
        return pl.ds(pl.multiple_of(slot * ROWS + c * SIZE, SIZE), SIZE)

    def move(src, dst, kind, wait_row, c, dev):
        cp = pltpu.make_async_remote_copy(
            src_ref=src, dst_ref=dst, send_sem=tsend.at[kind, c], recv_sem=trecv.at[wait_row, c],
            device_id=dev, device_id_type=MESH,
        )
        cp.start()
        made.append(cp)

    def send(kind, c):
        src, dst, wait_row, dev = kinds[kind]
        move(toks.at[rows_of(src, c)], toks.at[rows_of(dst, c)], kind, wait_row, c, dev)

    slot_of_row = (PAIR, NEAR + OWN, THIRD, NEAR + THIRD, NEAR + PAIR, None, FAR + OWN, FAR + PAIR, FAR + THIRD)

    def wait_in(ref, row, c):
        pltpu.make_async_remote_copy(
            src_ref=ref, dst_ref=ref, send_sem=tsend.at[row, c], recv_sem=trecv.at[row, c],
            device_id=dev_z, device_id_type=MESH,
        ).wait_recv()

    def arrived(row, c):
        wait_in(toks.at[rows_of(slot_of_row[row], c)], row, c)

    def send_pair(c):
        if c >= CHUNKS:
            return
        if c in RELAYED:
            move(toks.at[rows_of(OWN, c)], relayed.at[RELAYED.index(c)], 0, 9, c, relay_to)
        else:
            send(0, c)

    def pass_on(c):
        if c in RELAYED:
            buffer = relayed.at[RELAYED.index(c)]
            wait_in(buffer, 9, c)
            move(buffer, toks.at[rows_of(PAIR, c)], 9, 0, c, onward_to)

    def tick(i):
        if i < CHUNKS:
            pass_on(i + 2)
            arrived(0, i)
            send_pair(i + AHEAD)
            send(2, i)
            send(3, i)
            arrived(1, i)
            if i + NEAR_AHEAD < CHUNKS:
                send(1, i + NEAR_AHEAD)
            send(6, i)
        c = i - 1
        if 0 <= c < CHUNKS:
            arrived(2, c)
            arrived(3, c)
            send(4 if c % 2 == 0 else 5, c)
            send(8, c)
        c = i - 2
        if 0 <= c < CHUNKS:
            arrived(4, c)
            send(7, c)

    per = CHUNKS // PIECES
    ready = {}
    for p in range(PIECES):
        last = per * (p + 1) - 1
        ready[OWN, p] = 0
        ready[PAIR, p] = last
        ready[NEAR + OWN, p] = last
        ready[THIRD, p] = last + 1
        ready[NEAR + THIRD, p] = last + 1
        ready[NEAR + PAIR, p] = last + 2
        ready[FAR + OWN, p] = last + 4
        ready[FAR + THIRD, p] = last + 3
        ready[FAR + PAIR, p] = last + 4
    pending = sorted(ready, key=lambda k: (ready[k], k))

    def project(keys):
        offsets = []
        for slot, p in keys:
            if slot >= FAR:
                for c in range(per * p, per * (p + 1)):
                    arrived(slot, c)
            offsets.append(slot * PIECES + p)

        def body(k, carry):
            n = k % 2
            which = k // 2
            row = jnp.int32(offsets[0])
            for j in range(1, len(offsets)):
                row = jnp.where(which == j, offsets[j], row)
            rows = pl.ds(pl.multiple_of(row * PIECE, PIECE), PIECE)
            cols = pl.ds(pl.multiple_of(n * D, D), D)
            w = wkv[:, :, :, :, cols].reshape(D, D)
            kv[row, :, cols] = jnp.dot(
                toks[rows, :], w, preferred_element_type=jnp.float32
            ).astype(jnp.bfloat16)
            return carry

        lax.fori_loop(0, 2 * len(offsets), body, 0)

    def project_up_to(t, limit):
        keys = [k for k in pending if ready[k] <= t][:limit]
        for k in keys:
            pending.remove(k)
        if keys:
            project(keys)

    w_stage_z(0)
    for c in range(AHEAD):
        send_pair(c)
    w_stage_z(1)
    w_stage_x(0)
    for c in range(NEAR_AHEAD):
        send(1, c)
    pass_on(0)
    pass_on(1)
    w_stage_y(0)
    tick(0)
    w_stage_x(1)
    tick(1)
    w_stage_relay(0)
    w_stage_y(1)
    tick(2)
    w_stage_last(0)
    tick(3)
    w_ready(0)
    project_up_to(3, 8)
    tick(4)
    project_up_to(4, 8)
    w_stage_relay(1)
    tick(5)
    project_up_to(5, 8)
    w_stage_last(1)
    tick(6)
    project_up_to(6, 8)
    w_ready(1)

    def q_body(n, carry):
        cols = pl.ds(pl.multiple_of(n * 512, 512), 512)
        w = wqo[:, :, :, :, cols].reshape(D, 512)
        qs[:, cols] = jnp.dot(
            toks[pl.ds(0, ROWS), :], w, preferred_element_type=jnp.float32
        ).astype(jnp.bfloat16)
        return carry

    lax.fori_loop(0, 2, q_body, 0)
    tick(7)
    project_up_to(7, 8)
    tick(8)
    project_up_to(8, 8)
    tick(9)
    project_up_to(9, 36)
    project_up_to(10, 36)
    project_up_to(11, 36)

    ones = jnp.ones((NBR * BLK, HD), jnp.bfloat16)

    def one_head(h, carry):
        key_cols = pl.ds(pl.multiple_of(h * HD, HD), HD)
        value_cols = pl.ds(pl.multiple_of(h * HD + D, HD), HD)

        def score(b):
            q = qs[pl.ds(b * BLK, BLK), key_cols]
            keys = jnp.concatenate([kv[idx_ref[b, j], :, key_cols] for j in range(NBR)], axis=0)
            return lax.dot_general(
                q, keys, (((1,), (1,)), ((), ())), preferred_element_type=jnp.float32
            )

        def finish(b, scores):
            values = jnp.concatenate([kv[idx_ref[b, j], :, value_cols] for j in range(NBR)], axis=0)
            largest = jnp.max(scores, axis=-1, keepdims=True) * FACTOR
            expo = jnp.exp2(scores * FACTOR - largest).astype(jnp.bfloat16)
            both = jnp.dot(
                expo, jnp.concatenate([values, ones], axis=1), preferred_element_type=jnp.float32
            )
            att[pl.ds(b * BLK, BLK), key_cols] = (both[:, :HD] / both[:, HD:]).astype(jnp.bfloat16)

        scores = score(0)
        for b in range(1, ROWS // BLK):
            following = score(b)
            finish(b - 1, scores)
            scores = following
        finish(ROWS // BLK - 1, scores)
        return carry

    lax.fori_loop(0, HEADS, one_head, 0)

    def out_body(n, carry):
        cols = pl.ds(pl.multiple_of(n * 512, 512), 512)
        w = wqo[:, :, :, :, pl.ds(pl.multiple_of(D + n * 512, 512), 512)].reshape(D, 512)
        out_ref[:, cols] = jnp.dot(
            att[...], w, preferred_element_type=jnp.float32
        ).astype(jnp.bfloat16)
        return carry

    lax.fori_loop(0, 2, out_body, 0)
    for cp in made:
        cp.wait_send()
    for cp in made_w.values():
        cp.wait_send()


def layer(idx, tokens, w_qkv, w_out):
    vmem = pl.BlockSpec(memory_space=pltpu.VMEM)
    bf16 = jnp.bfloat16
    return pl.pallas_call(
        layer_kernel,
        out_shape=jax.ShapeDtypeStruct((ROWS, D), bf16),
        in_specs=[pl.BlockSpec(memory_space=pltpu.SMEM), vmem, vmem, vmem],
        out_specs=vmem,
        scratch_shapes=[
            pltpu.VMEM((SLOTS * ROWS, D), bf16),
            pltpu.VMEM((4, 4, 2, 32, 2 * D), bf16),
            pltpu.VMEM((4, 4, 2, 32, 2 * D), bf16),
            pltpu.VMEM((SLOTS * ROWS // BLK, BLK, 2 * D), bf16),
            pltpu.VMEM((ROWS, D), bf16),
            pltpu.VMEM((ROWS, D), bf16),
            pltpu.VMEM((len(RELAYED), SIZE, D), bf16),
            pltpu.SemaphoreType.DMA((10, CHUNKS)),
            pltpu.SemaphoreType.DMA((10, CHUNKS)),
            pltpu.SemaphoreType.DMA((2, 21)),
            pltpu.SemaphoreType.DMA((2, 21)),
        ],
        compiler_params=pltpu.CompilerParams(
            collective_id=0, has_side_effects=True, vmem_limit_bytes=56 << 20
        ),
        name="layer",
    )(idx, tokens, w_qkv, w_out)


def local_lists(neighbours):
    seq = lax.axis_index("seq")
    head = lax.axis_index("head")
    rows = ROWS // BLK
    lists = lax.dynamic_slice_in_dim(neighbours, head * rows, rows, axis=0)
    up = head // 4
    plane = seq * 2 + up
    row = head % 4
    depth = 64
    step = jnp.mod(lists // 16 - plane, depth)
    near = jnp.where(up == 0, 1, depth - 1)
    kind = jnp.where(step == 0, 0, jnp.where(step == near, 1, 2))
    y = (lists // 4) % 4
    pair = row + 1 - 2 * (row % 2)
    which = jnp.where(y == row, 0, jnp.where(y == pair, 1, 2))
    return ((kind * 3 + which) * 4 + lists % 4).astype(jnp.int32)


def local(tokens, w_qkv, w_out, neighbours):
    return layer(local_lists(neighbours), tokens, w_qkv, w_out)


def solution(mesh):
    return jax.shard_map(
        local,
        mesh=mesh,
        in_specs=(P(("seq", "head"), None), P("seq", None), P("seq", None), P("seq", None)),
        out_specs=P(("seq", "head"), None),
        check_vma=False,
    )
```

```python
import math

import jax
import jax.numpy as jnp
from jax import lax
from jax.experimental import pallas as pl
from jax.experimental.pallas import tpu as pltpu
from jax.sharding import PartitionSpec as P

HEADS = 8
HD = 128
BLK = 128
NBR = 12
ROWS = 512
D = 1024
SLOTS = 9
FACTOR = math.log2(math.e) / math.sqrt(HD)
MESH = pl.DeviceIdType.MESH
CHUNKS = 8
SIZE = ROWS // CHUNKS
PIECES = 4
PIECE = ROWS // PIECES
AHEAD = 3
NEAR_AHEAD = 3
RELAYED = (1, 4, 6)
OWN, PAIR, THIRD = 0, 1, 2
NEAR, FAR = 3, 6


def layer_kernel(idx_ref, tok_ref, wqkv_ref, wout_ref, out_ref,
                 toks, wkv, wqo, kv, qs, att,
                 relayed, tsend, trecv, wsend, wrecv):
    seq = lax.axis_index("seq")
    head = lax.axis_index("head")
    y = seq // 8
    zl = (seq // 2) % 4
    core = seq % 2
    x = head // 2
    zh = head % 2
    z = zh * 4 + zl
    up = x // 2

    def device(dx=0, dy=0, dz=0, dc=0):
        nz = lax.rem(z + dz + 8, 8)
        ny = lax.rem(y + dy + 4, 4)
        nx = lax.rem(x + dx + 4, 4)
        nc = lax.rem(core + dc, 2)
        return {"seq": ny * 8 + lax.rem(nz, 4) * 2 + nc, "head": nx * 2 + nz // 4}

    def at_x(low, high):
        nl = lax.rem(x % 2 + low, 2)
        nh = lax.rem(up + high, 2)
        return {"seq": seq, "head": (nh * 2 + nl) * 2 + zh}

    step = 1 - 2 * up
    dev_z = device(dz=4)
    dev_1, dev_2, dev_3 = at_x(1, 0), at_x(0, 1), at_x(1, 1)
    end = lax.rem(seq, 8)
    cross_to = jnp.where(end == 7 * (1 - up), 1, 0)
    cross_from = jnp.where(end == 7 * up, 1, 0)
    seq_to = lax.rem(seq + step + 32, 32)
    seq_from = lax.rem(seq - step + 32, 32)

    def across(seq_at, low, turn):
        return {"seq": seq_at, "head": (up * 2 + lax.rem(x % 2 + low, 2)) * 2 + lax.rem(zh + turn, 2)}

    far_to = across(seq_to, 0, cross_to)
    far_to_third = across(seq_to, cross_to, cross_to)
    far_from = across(seq_from, 0, cross_from)
    far_from_third = across(seq_from, cross_from, cross_from)
    relay_to, relay_from = device(dz=-step), device(dz=step)
    onward_to, onward_from = device(dz=-3 * step), device(dz=3 * step)
    w_z = (device(dz=1), device(dz=-1), device(dz=2))
    w_z_from = (device(dz=-1), device(dz=1), device(dz=-2))
    w_x = (device(dx=1), device(dx=-1), device(dx=2))
    w_y = (device(dy=1), device(dy=-1))
    sibling = device(dc=1)

    barrier = pltpu.get_barrier_semaphore()
    partners = (dev_z, dev_1, dev_2, dev_3, far_to, far_from, far_to_third, far_from_third)
    partners += (onward_to, onward_from) + w_z + w_z_from + w_x + w_y + (sibling,)
    for dev in partners:
        pl.semaphore_signal(barrier, inc=1, device_id=dev, device_id_type=MESH)

    wkv[y, zl, core] = wqkv_ref[:, D:]
    wqo[y, zl, core, :, :D] = wqkv_ref[:, :D]
    wqo[y, zl, core, :, D:] = wout_ref[...]
    toks[pl.ds(0, ROWS)] = tok_ref[...]
    pl.semaphore_wait(barrier, len(partners))

    weights = (wkv, wqo)
    quarter = pl.ds(pl.multiple_of(x * 512, 512), 512)
    made_w = {}

    def send_w(g, number, where, dev):
        cp = pltpu.make_async_remote_copy(
            src_ref=weights[g].at[where], dst_ref=weights[g].at[where],
            send_sem=wsend.at[g, number], recv_sem=wrecv.at[g, number],
            device_id=dev, device_id_type=MESH,
        )
        cp.start()
        made_w[g, number] = cp

    def got_w(g, *numbers):
        for number in numbers:
            made_w[g, number].wait_recv()

    every = slice(None)

    def w_stage_z(g):
        for j in range(3):
            send_w(g, j, (y, zl, core, every, quarter), w_z[j])

    def w_stage_x(g):
        for j, dz in enumerate((3, 1, 2)):
            got_w(g, j)
            for i in range(3):
                send_w(g, 3 + 3 * j + i, (y, lax.rem(zl + dz, 4), core, every, quarter), w_x[i])

    def w_stage_y(g):
        got_w(g, *range(3, 12))
        send_w(g, 12, (y, every, core), w_y[0])
        send_w(g, 13, (y, every, core), w_y[1])
        send_w(g, 16, (y, every, core), sibling)

    def w_stage_relay(g):
        down = lax.rem(y + 3, 4)
        above = lax.rem(y + 1, 4)
        got_w(g, 12)
        send_w(g, 14, (down, pl.ds(0, 2), core), w_y[0])
        send_w(g, 17, (down, every, core), sibling)
        got_w(g, 13)
        send_w(g, 15, (above, pl.ds(2, 2), core), w_y[1])
        send_w(g, 18, (above, every, core), sibling)

    def w_stage_last(g):
        across = lax.rem(y + 2, 4)
        got_w(g, 14)
        send_w(g, 19, (across, pl.ds(0, 2), core), sibling)
        got_w(g, 15)
        send_w(g, 20, (across, pl.ds(2, 2), core), sibling)

    def w_ready(g):
        got_w(g, *range(16, 21))

    kinds = {
        0: (OWN, PAIR, 0, dev_z),
        1: (OWN, NEAR + OWN, 1, dev_2),
        2: (PAIR, THIRD, 2, dev_1),
        3: (PAIR, NEAR + THIRD, 3, dev_3),
        4: (THIRD, NEAR + PAIR, 4, dev_3),
        5: (NEAR + THIRD, NEAR + PAIR, 4, dev_1),
        6: (NEAR + OWN, FAR + OWN + cross_to, 6 + cross_to, far_to),
        7: (NEAR + PAIR, FAR + PAIR - cross_to, 7 - cross_to, far_to),
        8: (NEAR + THIRD - 2 * cross_to, FAR + THIRD, 8, far_to_third),
    }
    made = []

    def rows_of(slot, c):
        return pl.ds(pl.multiple_of(slot * ROWS + c * SIZE, SIZE), SIZE)

    def move(src, dst, kind, wait_row, c, dev):
        cp = pltpu.make_async_remote_copy(
            src_ref=src, dst_ref=dst, send_sem=tsend.at[kind, c], recv_sem=trecv.at[wait_row, c],
            device_id=dev, device_id_type=MESH,
        )
        cp.start()
        made.append(cp)

    def send(kind, c):
        src, dst, wait_row, dev = kinds[kind]
        move(toks.at[rows_of(src, c)], toks.at[rows_of(dst, c)], kind, wait_row, c, dev)

    slot_of_row = (PAIR, NEAR + OWN, THIRD, NEAR + THIRD, NEAR + PAIR, None, FAR + OWN, FAR + PAIR, FAR + THIRD)

    def wait_in(ref, row, c):
        pltpu.make_async_remote_copy(
            src_ref=ref, dst_ref=ref, send_sem=tsend.at[row, c], recv_sem=trecv.at[row, c],
            device_id=dev_z, device_id_type=MESH,
        ).wait_recv()

    def arrived(row, c):
        wait_in(toks.at[rows_of(slot_of_row[row], c)], row, c)

    def send_pair(c):
        if c >= CHUNKS:
            return
        if c in RELAYED:
            move(toks.at[rows_of(OWN, c)], relayed.at[RELAYED.index(c)], 0, 9, c, relay_to)
        else:
            send(0, c)

    def pass_on(c):
        if c in RELAYED:
            buffer = relayed.at[RELAYED.index(c)]
            wait_in(buffer, 9, c)
            move(buffer, toks.at[rows_of(PAIR, c)], 9, 0, c, onward_to)

    def tick(i):
        if i < CHUNKS:
            pass_on(i + 2)
            arrived(0, i)
            send_pair(i + AHEAD)
            send(2, i)
            send(3, i)
            arrived(1, i)
            if i + NEAR_AHEAD < CHUNKS:
                send(1, i + NEAR_AHEAD)
            send(6, i)
        c = i - 1
        if 0 <= c < CHUNKS:
            arrived(2, c)
            arrived(3, c)
            send(4 if c % 2 == 0 else 5, c)
            send(8, c)
        c = i - 2
        if 0 <= c < CHUNKS:
            arrived(4, c)
            send(7, c)

    per = CHUNKS // PIECES
    ready = {}
    for p in range(PIECES):
        last = per * (p + 1) - 1
        ready[OWN, p] = 0
        ready[PAIR, p] = last
        ready[NEAR + OWN, p] = last
        ready[THIRD, p] = last + 1
        ready[NEAR + THIRD, p] = last + 1
        ready[NEAR + PAIR, p] = last + 2
        ready[FAR + OWN, p] = last + 4
        ready[FAR + THIRD, p] = last + 3
        ready[FAR + PAIR, p] = last + 4
    pending = sorted(ready, key=lambda k: (ready[k], k))

    def project(keys):
        offsets = []
        for slot, p in keys:
            if slot >= FAR:
                for c in range(per * p, per * (p + 1)):
                    arrived(slot, c)
            offsets.append(slot * PIECES + p)

        def body(k, carry):
            n = k % 2
            which = k // 2
            row = jnp.int32(offsets[0])
            for j in range(1, len(offsets)):
                row = jnp.where(which == j, offsets[j], row)
            rows = pl.ds(pl.multiple_of(row * PIECE, PIECE), PIECE)
            cols = pl.ds(pl.multiple_of(n * D, D), D)
            w = wkv[:, :, :, :, cols].reshape(D, D)
            kv[row, :, cols] = jnp.dot(
                toks[rows, :], w, preferred_element_type=jnp.float32
            ).astype(jnp.bfloat16)
            return carry

        lax.fori_loop(0, 2 * len(offsets), body, 0)

    def project_up_to(t, limit):
        keys = [k for k in pending if ready[k] <= t][:limit]
        for k in keys:
            pending.remove(k)
        if keys:
            project(keys)

    w_stage_z(0)
    w_stage_z(1)
    for c in range(AHEAD):
        send_pair(c)
    w_stage_x(0)
    for c in range(NEAR_AHEAD):
        send(1, c)
    pass_on(0)
    pass_on(1)
    w_stage_y(0)
    tick(0)
    w_stage_x(1)
    tick(1)
    w_stage_relay(0)
    w_stage_y(1)
    tick(2)
    w_stage_last(0)
    tick(3)
    w_ready(0)
    project_up_to(3, 8)
    tick(4)
    project_up_to(4, 8)
    w_stage_relay(1)
    tick(5)
    project_up_to(5, 8)
    w_stage_last(1)
    tick(6)
    project_up_to(6, 8)
    w_ready(1)

    def q_body(n, carry):
        cols = pl.ds(pl.multiple_of(n * 512, 512), 512)
        w = wqo[:, :, :, :, cols].reshape(D, 512)
        qs[:, cols] = jnp.dot(
            toks[pl.ds(0, ROWS), :], w, preferred_element_type=jnp.float32
        ).astype(jnp.bfloat16)
        return carry

    lax.fori_loop(0, 2, q_body, 0)
    tick(7)
    project_up_to(7, 8)
    tick(8)
    project_up_to(8, 8)
    tick(9)
    while pending:
        project_up_to(99, 3)

    ones = jnp.ones((NBR * BLK, HD), jnp.bfloat16)

    def one_head(h, carry):
        key_cols = pl.ds(pl.multiple_of(h * HD, HD), HD)
        value_cols = pl.ds(pl.multiple_of(h * HD + D, HD), HD)

        def score(b):
            q = qs[pl.ds(b * BLK, BLK), key_cols]
            keys = jnp.concatenate([kv[idx_ref[b, j], :, key_cols] for j in range(NBR)], axis=0)
            return lax.dot_general(
                q, keys, (((1,), (1,)), ((), ())), preferred_element_type=jnp.float32
            )

        def finish(b, scores):
            values = jnp.concatenate([kv[idx_ref[b, j], :, value_cols] for j in range(NBR)], axis=0)
            largest = jnp.max(scores, axis=-1, keepdims=True) * FACTOR
            expo = jnp.exp2(scores * FACTOR - largest).astype(jnp.bfloat16)
            both = jnp.dot(
                expo, jnp.concatenate([values, ones], axis=1), preferred_element_type=jnp.float32
            )
            att[pl.ds(b * BLK, BLK), key_cols] = (both[:, :HD] / both[:, HD:]).astype(jnp.bfloat16)

        scores = score(0)
        for b in range(1, ROWS // BLK):
            following = score(b)
            finish(b - 1, scores)
            scores = following
        finish(ROWS // BLK - 1, scores)
        return carry

    lax.fori_loop(0, HEADS, one_head, 0)

    def out_body(n, carry):
        cols = pl.ds(pl.multiple_of(n * 512, 512), 512)
        w = wqo[:, :, :, :, pl.ds(pl.multiple_of(D + n * 512, 512), 512)].reshape(D, 512)
        out_ref[:, cols] = jnp.dot(
            att[...], w, preferred_element_type=jnp.float32
        ).astype(jnp.bfloat16)
        return carry

    lax.fori_loop(0, 2, out_body, 0)
    for cp in made:
        cp.wait_send()
    for cp in made_w.values():
        cp.wait_send()


def layer(idx, tokens, w_qkv, w_out):
    vmem = pl.BlockSpec(memory_space=pltpu.VMEM)
    bf16 = jnp.bfloat16
    return pl.pallas_call(
        layer_kernel,
        out_shape=jax.ShapeDtypeStruct((ROWS, D), bf16),
        in_specs=[pl.BlockSpec(memory_space=pltpu.SMEM), vmem, vmem, vmem],
        out_specs=vmem,
        scratch_shapes=[
            pltpu.VMEM((SLOTS * ROWS, D), bf16),
            pltpu.VMEM((4, 4, 2, 32, 2 * D), bf16),
            pltpu.VMEM((4, 4, 2, 32, 2 * D), bf16),
            pltpu.VMEM((SLOTS * ROWS // BLK, BLK, 2 * D), bf16),
            pltpu.VMEM((ROWS, D), bf16),
            pltpu.VMEM((ROWS, D), bf16),
            pltpu.VMEM((len(RELAYED), SIZE, D), bf16),
            pltpu.SemaphoreType.DMA((10, CHUNKS)),
            pltpu.SemaphoreType.DMA((10, CHUNKS)),
            pltpu.SemaphoreType.DMA((2, 21)),
            pltpu.SemaphoreType.DMA((2, 21)),
        ],
        compiler_params=pltpu.CompilerParams(
            collective_id=0, has_side_effects=True, vmem_limit_bytes=56 << 20
        ),
        name="layer",
    )(idx, tokens, w_qkv, w_out)


def local_lists(neighbours):
    seq = lax.axis_index("seq")
    head = lax.axis_index("head")
    rows = ROWS // BLK
    lists = lax.dynamic_slice_in_dim(neighbours, head * rows, rows, axis=0)
    up = head // 4
    plane = seq * 2 + up
    row = head % 4
    depth = 64
    step = jnp.mod(lists // 16 - plane, depth)
    near = jnp.where(up == 0, 1, depth - 1)
    kind = jnp.where(step == 0, 0, jnp.where(step == near, 1, 2))
    y = (lists // 4) % 4
    pair = row + 1 - 2 * (row % 2)
    which = jnp.where(y == row, 0, jnp.where(y == pair, 1, 2))
    return ((kind * 3 + which) * 4 + lists % 4).astype(jnp.int32)


def local(tokens, w_qkv, w_out, neighbours):
    return layer(local_lists(neighbours), tokens, w_qkv, w_out)


def solution(mesh):
    return jax.shard_map(
        local,
        mesh=mesh,
        in_specs=(P(("seq", "head"), None), P("seq", None), P("seq", None), P("seq", None)),
        out_specs=P(("seq", "head"), None),
        check_vma=False,
    )
```

```python
import math

import jax
import jax.numpy as jnp
from jax import lax
from jax.experimental import pallas as pl
from jax.experimental.pallas import tpu as pltpu
from jax.sharding import PartitionSpec as P

HEADS = 8
HD = 128
BLK = 128
NBR = 12
ROWS = 512
D = 1024
SLOTS = 9
FACTOR = math.log2(math.e) / math.sqrt(HD)
MESH = pl.DeviceIdType.MESH
CHUNKS = 8
SIZE = ROWS // CHUNKS
PIECES = 4
PIECE = ROWS // PIECES
AHEAD = 3
NEAR_AHEAD = 3
RELAYED = (1, 4, 6)
OWN, PAIR, THIRD = 0, 1, 2
NEAR, FAR = 3, 6


def layer_kernel(idx_ref, tok_ref, wqkv_ref, wout_ref, out_ref,
                 toks, wkv, wqo, kv, qs, att,
                 relayed, tsend, trecv, wsend, wrecv):
    seq = lax.axis_index("seq")
    head = lax.axis_index("head")
    y = seq // 8
    zl = (seq // 2) % 4
    core = seq % 2
    x = head // 2
    zh = head % 2
    z = zh * 4 + zl
    up = x // 2

    def device(dx=0, dy=0, dz=0, dc=0):
        nz = lax.rem(z + dz + 8, 8)
        ny = lax.rem(y + dy + 4, 4)
        nx = lax.rem(x + dx + 4, 4)
        nc = lax.rem(core + dc, 2)
        return {"seq": ny * 8 + lax.rem(nz, 4) * 2 + nc, "head": nx * 2 + nz // 4}

    def at_x(low, high):
        nl = lax.rem(x % 2 + low, 2)
        nh = lax.rem(up + high, 2)
        return {"seq": seq, "head": (nh * 2 + nl) * 2 + zh}

    step = 1 - 2 * up
    dev_z = device(dz=4)
    dev_1, dev_2, dev_3 = at_x(1, 0), at_x(0, 1), at_x(1, 1)
    end = lax.rem(seq, 8)
    cross_to = jnp.where(end == 7 * (1 - up), 1, 0)
    cross_from = jnp.where(end == 7 * up, 1, 0)
    seq_to = lax.rem(seq + step + 32, 32)
    seq_from = lax.rem(seq - step + 32, 32)

    def across(seq_at, low, turn):
        return {"seq": seq_at, "head": (up * 2 + lax.rem(x % 2 + low, 2)) * 2 + lax.rem(zh + turn, 2)}

    far_to = across(seq_to, 0, cross_to)
    far_to_third = across(seq_to, cross_to, cross_to)
    far_from = across(seq_from, 0, cross_from)
    far_from_third = across(seq_from, cross_from, cross_from)
    relay_to, relay_from = device(dz=-step), device(dz=step)
    onward_to, onward_from = device(dz=-3 * step), device(dz=3 * step)
    w_z = (device(dz=1), device(dz=-1), device(dz=2))
    w_z_from = (device(dz=-1), device(dz=1), device(dz=-2))
    w_x = (device(dx=1), device(dx=-1), device(dx=2))
    w_y = (device(dy=1), device(dy=-1))
    sibling = device(dc=1)

    barrier = pltpu.get_barrier_semaphore()
    partners = (dev_z, dev_1, dev_2, dev_3, far_to, far_from, far_to_third, far_from_third)
    partners += (onward_to, onward_from) + w_z + w_z_from + w_x + w_y + (sibling,)
    for dev in partners:
        pl.semaphore_signal(barrier, inc=1, device_id=dev, device_id_type=MESH)

    wkv[y, zl, core] = wqkv_ref[:, D:]
    wqo[y, zl, core, :, :D] = wqkv_ref[:, :D]
    wqo[y, zl, core, :, D:] = wout_ref[...]
    toks[pl.ds(0, ROWS)] = tok_ref[...]
    pl.semaphore_wait(barrier, len(partners))

    weights = (wkv, wqo)
    quarter = pl.ds(pl.multiple_of(x * 512, 512), 512)
    made_w = {}

    def send_w(g, number, where, dev):
        cp = pltpu.make_async_remote_copy(
            src_ref=weights[g].at[where], dst_ref=weights[g].at[where],
            send_sem=wsend.at[g, number], recv_sem=wrecv.at[g, number],
            device_id=dev, device_id_type=MESH,
        )
        cp.start()
        made_w[g, number] = cp

    def got_w(g, *numbers):
        for number in numbers:
            made_w[g, number].wait_recv()

    every = slice(None)

    def w_stage_z(g):
        for j in range(3):
            send_w(g, j, (y, zl, core, every, quarter), w_z[j])

    def w_stage_x(g):
        for j, dz in enumerate((3, 1, 2)):
            got_w(g, j)
            for i in range(3):
                send_w(g, 3 + 3 * j + i, (y, lax.rem(zl + dz, 4), core, every, quarter), w_x[i])

    def w_stage_y(g):
        got_w(g, *range(3, 12))
        send_w(g, 12, (y, every, core), w_y[0])
        send_w(g, 13, (y, every, core), w_y[1])
        send_w(g, 16, (y, every, core), sibling)

    def w_stage_relay(g):
        down = lax.rem(y + 3, 4)
        above = lax.rem(y + 1, 4)
        got_w(g, 12)
        send_w(g, 14, (down, pl.ds(0, 2), core), w_y[0])
        send_w(g, 17, (down, every, core), sibling)
        got_w(g, 13)
        send_w(g, 15, (above, pl.ds(2, 2), core), w_y[1])
        send_w(g, 18, (above, every, core), sibling)

    def w_stage_last(g):
        across = lax.rem(y + 2, 4)
        got_w(g, 14)
        send_w(g, 19, (across, pl.ds(0, 2), core), sibling)
        got_w(g, 15)
        send_w(g, 20, (across, pl.ds(2, 2), core), sibling)

    def w_ready(g):
        got_w(g, *range(16, 21))

    kinds = {
        0: (OWN, PAIR, 0, dev_z),
        1: (OWN, NEAR + OWN, 1, dev_2),
        2: (PAIR, THIRD, 2, dev_1),
        3: (PAIR, NEAR + THIRD, 3, dev_3),
        4: (THIRD, NEAR + PAIR, 4, dev_3),
        5: (NEAR + THIRD, NEAR + PAIR, 4, dev_1),
        6: (NEAR + OWN, FAR + OWN + cross_to, 6 + cross_to, far_to),
        7: (NEAR + PAIR, FAR + PAIR - cross_to, 7 - cross_to, far_to),
        8: (NEAR + THIRD - 2 * cross_to, FAR + THIRD, 8, far_to_third),
    }
    made = []

    def rows_of(slot, c):
        return pl.ds(pl.multiple_of(slot * ROWS + c * SIZE, SIZE), SIZE)

    def move(src, dst, kind, wait_row, c, dev):
        cp = pltpu.make_async_remote_copy(
            src_ref=src, dst_ref=dst, send_sem=tsend.at[kind, c], recv_sem=trecv.at[wait_row, c],
            device_id=dev, device_id_type=MESH,
        )
        cp.start()
        made.append(cp)

    def send(kind, c):
        src, dst, wait_row, dev = kinds[kind]
        move(toks.at[rows_of(src, c)], toks.at[rows_of(dst, c)], kind, wait_row, c, dev)

    slot_of_row = (PAIR, NEAR + OWN, THIRD, NEAR + THIRD, NEAR + PAIR, None, FAR + OWN, FAR + PAIR, FAR + THIRD)

    def wait_in(ref, row, c):
        pltpu.make_async_remote_copy(
            src_ref=ref, dst_ref=ref, send_sem=tsend.at[row, c], recv_sem=trecv.at[row, c],
            device_id=dev_z, device_id_type=MESH,
        ).wait_recv()

    def arrived(row, c):
        wait_in(toks.at[rows_of(slot_of_row[row], c)], row, c)

    def send_pair(c):
        if c >= CHUNKS:
            return
        if c in RELAYED:
            move(toks.at[rows_of(OWN, c)], relayed.at[RELAYED.index(c)], 0, 9, c, relay_to)
        else:
            send(0, c)

    def pass_on(c):
        if c in RELAYED:
            buffer = relayed.at[RELAYED.index(c)]
            wait_in(buffer, 9, c)
            move(buffer, toks.at[rows_of(PAIR, c)], 9, 0, c, onward_to)

    def tick(i):
        if i < CHUNKS:
            pass_on(i + 2)
            arrived(0, i)
            send_pair(i + AHEAD)
            send(2, i)
            send(3, i)
            arrived(1, i)
            if i + NEAR_AHEAD < CHUNKS:
                send(1, i + NEAR_AHEAD)
            send(6, i)
        c = i - 1
        if 0 <= c < CHUNKS:
            arrived(2, c)
            arrived(3, c)
            send(4 if c % 2 == 0 else 5, c)
            send(8, c)
        c = i - 2
        if 0 <= c < CHUNKS:
            arrived(4, c)
            send(7, c)

    per = CHUNKS // PIECES
    ready = {}
    for p in range(PIECES):
        last = per * (p + 1) - 1
        ready[OWN, p] = 0
        ready[PAIR, p] = last
        ready[NEAR + OWN, p] = last
        ready[THIRD, p] = last + 1
        ready[NEAR + THIRD, p] = last + 1
        ready[NEAR + PAIR, p] = last + 2
        ready[FAR + OWN, p] = last + 4
        ready[FAR + THIRD, p] = last + 3
        ready[FAR + PAIR, p] = last + 4
    pending = sorted(ready, key=lambda k: (ready[k], k))

    def project(keys):
        offsets = []
        for slot, p in keys:
            if slot >= FAR:
                for c in range(per * p, per * (p + 1)):
                    arrived(slot, c)
            offsets.append(slot * PIECES + p)

        def body(k, carry):
            n = k % 2
            which = k // 2
            row = jnp.int32(offsets[0])
            for j in range(1, len(offsets)):
                row = jnp.where(which == j, offsets[j], row)
            rows = pl.ds(pl.multiple_of(row * PIECE, PIECE), PIECE)
            cols = pl.ds(pl.multiple_of(n * D, D), D)
            w = wkv[:, :, :, :, cols].reshape(D, D)
            kv[row, :, cols] = jnp.dot(
                toks[rows, :], w, preferred_element_type=jnp.float32
            ).astype(jnp.bfloat16)
            return carry

        lax.fori_loop(0, 2 * len(offsets), body, 0)

    def project_up_to(t, limit):
        keys = [k for k in pending if ready[k] <= t][:limit]
        for k in keys:
            pending.remove(k)
        if keys:
            project(keys)

    w_stage_z(0)
    for c in range(AHEAD):
        send_pair(c)
    w_stage_z(1)
    w_stage_x(0)
    for c in range(NEAR_AHEAD):
        send(1, c)
    pass_on(0)
    pass_on(1)
    w_stage_y(0)
    tick(0)
    w_stage_x(1)
    tick(1)
    w_stage_relay(0)
    w_stage_y(1)
    tick(2)
    w_stage_last(0)
    tick(3)
    w_ready(0)
    project_up_to(3, 8)
    tick(4)
    project_up_to(4, 8)
    w_stage_relay(1)
    tick(5)
    project_up_to(5, 8)
    w_stage_last(1)
    tick(6)
    project_up_to(6, 8)
    w_ready(1)

    def q_body(n, carry):
        cols = pl.ds(pl.multiple_of(n * 512, 512), 512)
        w = wqo[:, :, :, :, cols].reshape(D, 512)
        qs[:, cols] = jnp.dot(
            toks[pl.ds(0, ROWS), :], w, preferred_element_type=jnp.float32
        ).astype(jnp.bfloat16)
        return carry

    lax.fori_loop(0, 2, q_body, 0)
    tick(7)
    project_up_to(7, 8)
    tick(8)
    project_up_to(8, 8)
    tick(9)
    while pending:
        project_up_to(99, 3)

    ones = jnp.ones((NBR * BLK, HD), jnp.bfloat16)

    def one_head(h, carry):
        key_cols = pl.ds(pl.multiple_of(h * HD, HD), HD)
        value_cols = pl.ds(pl.multiple_of(h * HD + D, HD), HD)

        def score(b):
            q = qs[pl.ds(b * BLK, BLK), key_cols]
            keys = jnp.concatenate([kv[idx_ref[b, j], :, key_cols] for j in range(NBR)], axis=0)
            return lax.dot_general(
                q, keys, (((1,), (1,)), ((), ())), preferred_element_type=jnp.float32
            )

        def finish(b, scores):
            values = jnp.concatenate([kv[idx_ref[b, j], :, value_cols] for j in range(NBR)], axis=0)
            largest = jnp.max(scores, axis=-1, keepdims=True) * FACTOR
            expo = jnp.exp2(scores * FACTOR - largest).astype(jnp.bfloat16)
            both = jnp.dot(
                expo, jnp.concatenate([values, ones], axis=1), preferred_element_type=jnp.float32
            )
            att[pl.ds(b * BLK, BLK), key_cols] = (both[:, :HD] / both[:, HD:]).astype(jnp.bfloat16)

        scores = score(0)
        for b in range(1, ROWS // BLK):
            following = score(b)
            finish(b - 1, scores)
            scores = following
        finish(ROWS // BLK - 1, scores)
        return carry

    lax.fori_loop(0, HEADS, one_head, 0)

    def out_body(n, carry):
        cols = pl.ds(pl.multiple_of(n * 512, 512), 512)
        w = wqo[:, :, :, :, pl.ds(pl.multiple_of(D + n * 512, 512), 512)].reshape(D, 512)
        out_ref[:, cols] = jnp.dot(
            att[...], w, preferred_element_type=jnp.float32
        ).astype(jnp.bfloat16)
        return carry

    lax.fori_loop(0, 2, out_body, 0)
    for cp in made:
        cp.wait_send()
    for cp in made_w.values():
        cp.wait_send()


def layer(idx, tokens, w_qkv, w_out):
    vmem = pl.BlockSpec(memory_space=pltpu.VMEM)
    bf16 = jnp.bfloat16
    return pl.pallas_call(
        layer_kernel,
        out_shape=jax.ShapeDtypeStruct((ROWS, D), bf16),
        in_specs=[pl.BlockSpec(memory_space=pltpu.SMEM), vmem, vmem, vmem],
        out_specs=vmem,
        scratch_shapes=[
            pltpu.VMEM((SLOTS * ROWS, D), bf16),
            pltpu.VMEM((4, 4, 2, 32, 2 * D), bf16),
            pltpu.VMEM((4, 4, 2, 32, 2 * D), bf16),
            pltpu.VMEM((SLOTS * ROWS // BLK, BLK, 2 * D), bf16),
            pltpu.VMEM((ROWS, D), bf16),
            pltpu.VMEM((ROWS, D), bf16),
            pltpu.VMEM((len(RELAYED), SIZE, D), bf16),
            pltpu.SemaphoreType.DMA((10, CHUNKS)),
            pltpu.SemaphoreType.DMA((10, CHUNKS)),
            pltpu.SemaphoreType.DMA((2, 21)),
            pltpu.SemaphoreType.DMA((2, 21)),
        ],
        compiler_params=pltpu.CompilerParams(
            collective_id=0, has_side_effects=True, vmem_limit_bytes=56 << 20
        ),
        name="layer",
    )(idx, tokens, w_qkv, w_out)


def local_lists(neighbours):
    seq = lax.axis_index("seq")
    head = lax.axis_index("head")
    rows = ROWS // BLK
    lists = lax.dynamic_slice_in_dim(neighbours, head * rows, rows, axis=0)
    up = head // 4
    plane = seq * 2 + up
    row = head % 4
    depth = 64
    step = jnp.mod(lists // 16 - plane, depth)
    near = jnp.where(up == 0, 1, depth - 1)
    kind = jnp.where(step == 0, 0, jnp.where(step == near, 1, 2))
    y = (lists // 4) % 4
    pair = row + 1 - 2 * (row % 2)
    which = jnp.where(y == row, 0, jnp.where(y == pair, 1, 2))
    return ((kind * 3 + which) * 4 + lists % 4).astype(jnp.int32)


def local(tokens, w_qkv, w_out, neighbours):
    return layer(local_lists(neighbours), tokens, w_qkv, w_out)


def solution(mesh):
    return jax.shard_map(
        local,
        mesh=mesh,
        in_specs=(P(("seq", "head"), None), P("seq", None), P("seq", None), P("seq", None)),
        out_specs=P(("seq", "head"), None),
        check_vma=False,
    )
```
